32 devices in a mesh: slab: 8 (over z, y), grp: 4 (over x, core).
Axes of the slice: x: 2, y: 2, z: 4, core: 2. Of those that a mesh axis runs over, the one named last changes fastest.
Arguments:
- potential: bfloat16 [64, 8, 1024], P('slab'), may hold values from -3 to 3
- coefficients: bfloat16 [128, 16, 8, 1024], P(('slab', 'grp')), may hold values from -1 to 1
- box_center: int32 [128], replicated, may hold values from 0 to 63, as said below
- box_extent: int32 [128], replicated, may hold values from 8 to 16
Outputs:
- margin: float32 [128, 80], P(('slab', 'grp'))
- hamiltonian: float32 [128, 80], P(('slab', 'grp'))
The draws below stay inside these ranges and needn't reach their ends.
Inputs may be any that keep to these rules, and one draw needn't show every extreme that they name: `box_center`: function b's centre lies among the 8 planes of slab b // 16, that is from (8 * (b // 16)) on.
All inputs are finite; a program needn't handle non-finite values.
Results may differ from the reference program's by a relative error of at most 0.0003.
Values may be sent and summed in bfloat16 or wider, within the bound.
A program may use at most 64 MiB of HBM per device.

```python
import jax
import jax.numpy as jnp
from jax import lax

SZ = 8
EMAX = 16
COMP = 8
CX = 32
CY = 32
HW = 8
CS = 1024
NZ = 64
MEMBERS = 16
FUNCS = 128
BAND = 80
N_SLAB = 8


def draw_coefficients(key, part):
    keys = jax.random.split(jax.random.fold_in(key, 17), 3)
    centre_x = jax.random.uniform(keys[0], (FUNCS, 1), minval=0.0, maxval=float(CX))
    centre_y = jax.random.uniform(keys[1], (FUNCS, 1), minval=0.0, maxval=float(CY))
    cells = jnp.arange(CX * CY)
    cell_x = (cells // CY).astype(jnp.float32)[None, :]
    cell_y = (cells % CY).astype(jnp.float32)[None, :]
    delta_x = cell_x - centre_x
    delta_y = cell_y - centre_y
    envelope = 0.05 + jnp.exp(-(delta_x * delta_x + delta_y * delta_y) / 4.5)
    energy = jnp.sum(envelope * envelope, axis=1, keepdims=True)
    amplitude = 1.0 / jnp.sqrt(energy * float(EMAX * COMP))
    shape = (FUNCS, EMAX, COMP, CX * CY)
    base = jax.random.truncated_normal(keys[2], -6.0, 6.0, shape)
    values = base * (amplitude * envelope)[:, None, None, :]
    return values.astype(jnp.bfloat16)


def draw_box_center(key, part):
    offsets = jax.random.randint(jax.random.fold_in(key, 29), (FUNCS,), 0, SZ)
    owner = jnp.arange(FUNCS, dtype=jnp.int32) // (FUNCS // N_SLAB)
    return (owner * SZ + offsets).astype(jnp.int32)


def plant(array, own_key, low, largest):
    index_at = [jax.random.randint(jax.random.fold_in(own_key, axis), (), 0, length) for axis, length in enumerate(array.shape)]
    widest = array.shape.index(max(array.shape))
    next_to = index_at[:widest] + [(index_at[widest] + 1) % array.shape[widest]] + index_at[widest + 1:]
    return array.at[tuple(index_at)].set(low).at[tuple(next_to)].set(largest)


def levels(stream_key, dims, cuts, smallest, largest):
    def one(axis_at, blocks):
        draws = jax.random.uniform(jax.random.fold_in(jax.random.fold_in(stream_key, 6), axis_at), (blocks,), jnp.float32, smallest / len(cuts), largest / len(cuts))
        return jnp.repeat(jnp.exp(draws), dims[axis_at] // blocks).reshape((-1,) + (1,) * (len(dims) - axis_at - 1))

    loudness = one(*cuts[0])
    for cut in cuts[1:]:
        loudness = loudness * one(*cut)
    return loudness


def setup_inputs(seed: int = 0) -> dict:
    key_of = jax.random.split(jax.random.key(seed), 5)
    return {
        "potential": jnp.clip(jax.random.uniform(key_of[0], (NZ, COMP, CS), jnp.float32, -3.0, 3.0) * levels(key_of[0], (NZ, COMP, CS), ((0, 8),), -0.4, 0.0), -3.0, 3.0).astype(jnp.bfloat16),
        "coefficients": draw_coefficients(jax.random.fold_in(key_of[4], 71), 0),
        "box_center": draw_box_center(jax.random.fold_in(key_of[4], 71), 0),
        "box_extent": plant(jax.random.randint(key_of[3], (FUNCS,), EMAX // 2, EMAX + 1), jax.random.fold_in(key_of[3], 1), EMAX // 2, EMAX).astype(jnp.int32),
    }


def haar_signs():
    row_ids = jnp.arange(COMP, dtype=jnp.int32)[:, None]
    col_ids = jnp.arange(COMP, dtype=jnp.int32)[None, :]
    common = jnp.bitwise_and(row_ids, col_ids)
    parity = (common % 2 + (common // 2) % 2 + (common // 4) % 2) % 2
    return (1 - 2 * parity).astype(jnp.float32)


def apply_hamiltonian(orbital, pot_box, inside):
    shaped = orbital.reshape(orbital.shape[:3] + (CX, CY))
    bordered = jnp.pad(shaped, ((0, 0), (0, 0), (0, 0), (1, 1), (1, 1)))
    beside_all = bordered[:, :, :, 2:, 1:-1] + bordered[:, :, :, :-2, 1:-1] + bordered[:, :, :, 1:-1, 2:] + bordered[:, :, :, 1:-1, :-2]
    plane_term = (2.0 * shaped - 0.5 * beside_all).reshape(orbital.shape)
    padded = jnp.pad(orbital, ((0, 0), (1, 1), (0, 0), (0, 0)))
    depth_term = orbital - 0.5 * (padded[:, :-2] + padded[:, 2:])
    haar_table = haar_signs()
    fine_values = jnp.einsum("kc,npcx->npkx", haar_table, orbital, precision=lax.Precision.HIGHEST)
    potential_term = jnp.einsum("kc,npkx->npcx", haar_table, pot_box * fine_values, precision=lax.Precision.HIGHEST) / COMP
    return jnp.where(inside, plane_term + depth_term + potential_term, 0.0).astype(jnp.bfloat16)


def place_planes(starts, frame_depth, tile_data):
    source = jnp.arange(EMAX, dtype=jnp.int32)
    target = jnp.arange(frame_depth, dtype=jnp.int32)
    onehot = (starts[:, None, None] + source[None, None, :] == target[None, :, None]).astype(jnp.float32)
    return jnp.einsum("nqp,npcx->nqcx", onehot, tile_data, precision=lax.Precision.HIGHEST)


def reference(potential, coefficients, box_center, box_extent):
    frame_depth = SZ + EMAX
    planes = jnp.arange(EMAX, dtype=jnp.int32)
    member_ids = jnp.arange(MEMBERS, dtype=jnp.int32)
    steps_away = jnp.arange(5, dtype=jnp.int32) - 2

    def per_slab(slab_index):
        band_slabs = (slab_index + steps_away) % N_SLAB
        band_rows = (band_slabs[:, None] * MEMBERS + member_ids[None, :]).reshape(-1)
        centers = jnp.take(box_center, band_rows)
        extents = jnp.take(box_extent, band_rows)
        shifts = jnp.repeat(steps_away, MEMBERS, total_repeat_length=BAND)
        home = jnp.repeat(band_slabs, MEMBERS, total_repeat_length=BAND)
        relative = centers - home * SZ + shifts * SZ - extents // 2 + HW
        inside = planes[None, :] < extents[:, None]
        values = jnp.take(coefficients, band_rows, axis=0).astype(jnp.float32)
        orbital = jnp.where(inside[:, :, None, None], values, 0.0)
        window = place_planes(relative, frame_depth, orbital)
        own_orbital = orbital[2 * MEMBERS:3 * MEMBERS]
        own_relative = relative[2 * MEMBERS:3 * MEMBERS]
        own_inside = inside[2 * MEMBERS:3 * MEMBERS]
        plane_ids = (slab_index * SZ + own_relative - HW)[:, None] + planes[None, :]
        pot_box = jnp.take(potential, plane_ids % NZ, axis=0).astype(jnp.float32)
        applied = apply_hamiltonian(own_orbital, pot_box, own_inside[:, :, None, None])
        applied_window = place_planes(own_relative, frame_depth, applied.astype(jnp.float32))
        flat_window = window.reshape(window.shape[0], -1)
        own_window = window[2 * MEMBERS:3 * MEMBERS].reshape(MEMBERS, -1)
        margin_rows = jnp.dot(own_window, flat_window.T, precision=lax.Precision.HIGHEST)
        ham_rows = jnp.dot(applied_window.reshape(MEMBERS, -1), flat_window.T, precision=lax.Precision.HIGHEST)
        return margin_rows, ham_rows

    margin, hamiltonian = lax.map(per_slab, jnp.arange(N_SLAB, dtype=jnp.int32))
    return margin.reshape(FUNCS, BAND), hamiltonian.reshape(FUNCS, BAND)
```

```python
import functools

import jax
import jax.numpy as jnp
import numpy as np
from jax import lax
from jax.experimental import pallas as pl
from jax.experimental.pallas import tpu as pltpu
from jax.sharding import PartitionSpec as P

COMP = 8
CX = 32
CY = 32
MESH = pl.DeviceIdType.MESH


def haar_signs():
    ids = np.arange(COMP)
    common = ids[:, None] & ids[None, :]
    parity = (common % 2 + common // 2 % 2 + common // 4 % 2) % 2
    return (1 - 2 * parity).astype(np.float32)


def matrices(members, per, seg):
    rows = members * COMP
    order = np.zeros((COMP, members, members, COMP), np.float32)
    haar = np.zeros((COMP, members, members, COMP), np.float32)
    signs = haar_signs()
    half = per // 2
    pick = np.zeros((COMP, members, members // 2, COMP), np.float32)
    for n in range(members):
        group, func = divmod(n, per)
        for c in range(COMP):
            order[c, n, n, c] = 1.0
            haar[c, n, n, :] = signs[c]
            pick[c, n, group * half + func % half, c] = 1.0
    stacked = np.concatenate([order.reshape(rows, rows), haar.reshape(rows, rows)], 0)
    lap = np.zeros((seg + 128, seg), np.float32)
    for i in range(seg):
        lap[i, i] = 3.0
        if i % CY:
            lap[i - 1, i] = -0.5
            lap[i, i - 1] = -0.5
        if i >= CY:
            lap[i - CY, i] = -0.5
            lap[i, i - CY] = -0.5
    for i in range(CY):
        lap[seg + 128 - CY + i, i] = -0.5
        lap[seg + 64 - CY + i, i] = -0.5
        lap[seg + i, seg - CY + i] = -0.5
        lap[seg + 64 + i, seg - CY + i] = -0.5
    as_bf16 = lambda value: jnp.asarray(value, jnp.bfloat16)
    return as_bf16(stacked), as_bf16(pick.reshape(rows, -1)), as_bf16(lap)


def frame_kernel(groups, depth, scal_ref, coef_ref, main_ref, halo_ref):
    per, box, comp, cells = coef_ref.shape
    seg = cells // groups
    half = per // 2
    lane = lax.broadcasted_iota(jnp.int32, (comp, 128), 1)
    for sec in range(3):
        base = scal_ref[sec]

        @pl.loop(0, depth + 2 if sec == 1 else depth + 1)
        def _(j):
            planes = []
            for f in range(per):
                p = base + j - scal_ref[3 + f]
                inside = (p >= 0) & (p < scal_ref[3 + per + f])
                value = coef_ref[f, jnp.clip(p, 0, box - 1)].astype(jnp.float32)
                planes.append(jnp.where(inside, value, 0.0))
            for g in range(groups):
                at = slice(g * seg, (g + 1) * seg)
                main_ref[sec, g, j] = jnp.concatenate([v[:, at] for v in planes], 0).astype(
                    jnp.bfloat16
                )
                tiles = []
                for v in planes:
                    zero = jnp.zeros((comp, 128), jnp.float32)
                    before = v[:, g * seg - 128 : g * seg] if g else zero
                    after = (
                        v[:, (g + 1) * seg : (g + 1) * seg + 128] if g < groups - 1 else zero
                    )
                    tiles.append(
                        jnp.where(lane >= 128 - CY, before, jnp.where(lane < CY, after, 0.0))
                    )
                packed = [
                    tiles[f] + pltpu.roll(tiles[half + f], 64, 1) for f in range(half)
                ]
                halo_ref[sec, g, j] = jnp.concatenate(packed, 0).astype(jnp.bfloat16)


def band_kernel(
    slabs,
    groups,
    depth,
    per,
    seg,
    main_ref,
    halo_ref,
    pot_ref,
    mask_ref,
    order_ref,
    pick_ref,
    lap_ref,
    margin_ref,
    ham_ref,
    got,
    got_halo,
    got_pot,
    orb,
    app,
    rows,
    got_rows,
    send_main,
    send_halo,
    send_pot,
    send_rows,
    recv_main,
    recv_halo,
    recv_pot,
    recv_rows,
):
    slab = lax.axis_index("slab")
    me = lax.axis_index("grp")
    members = groups * per
    odd = lax.rem(slab, 2)
    partner = slab + 1 - 2 * odd
    ahead = lax.rem(slab + 2, slabs)
    behind = lax.rem(slab + slabs - 2, slabs)
    frame_to = [slab, partner, lax.select(odd == 1, ahead, behind)]
    rows_to = [slab, partner, lax.select(odd == 1, behind, ahead)]
    slots = [2 * odd, 1, 2 - 2 * odd]
    shifts = [odd, 0, 1 - odd]
    counts = [depth + 1, depth + 2, depth + 1]

    @pl.loop(0, groups)
    def _(g):
        for slot in (0, 2):
            for plane in (0, depth + 1):
                got[slot, g, plane] = jnp.zeros(got.shape[3:], got.dtype)
                got_halo[slot, g, plane] = jnp.zeros(got_halo.shape[3:], got_halo.dtype)

    barrier = pltpu.get_barrier_semaphore()
    for step in range(groups):
        to = lax.rem(me + step, groups)
        for place in (slab, partner, ahead, behind):
            if place is slab and step == 0:
                continue
            pl.semaphore_signal(barrier, inc=1, device_id=(place, to), device_id_type=MESH)
    pl.semaphore_wait(barrier, 4 * groups - 1)

    def frame_copies(sec, step):
        to = lax.rem(me + step, groups)
        count, slot, shift = counts[sec], slots[sec], shifts[sec]
        out = []
        for src, dst, send, recv in (
            (main_ref, got, send_main, recv_main),
            (halo_ref, got_halo, send_halo, recv_halo),
        ):
            source = src.at[sec, to, pl.ds(0, count)]
            target = dst.at[slot, me, pl.ds(shift, count)]
            if sec == 0 and step == 0:
                out.append(pltpu.make_async_copy(source, target, recv.at[sec, me]))
            else:
                out.append(
                    pltpu.make_async_remote_copy(
                        src_ref=source,
                        dst_ref=target,
                        send_sem=send.at[sec, step],
                        recv_sem=recv.at[sec, me],
                        device_id=(frame_to[sec], to),
                        device_id_type=MESH,
                    )
                )
        return out

    pot_copy = pltpu.make_async_remote_copy(
        src_ref=pot_ref.at[:, :, pl.ds(pl.multiple_of(me * seg, seg), seg)],
        dst_ref=got_pot,
        send_sem=send_pot,
        recv_sem=recv_pot,
        device_id=(partner, me),
        device_id_type=MESH,
    )
    pot_copy.start()
    sent = []
    for step in range(groups):
        for sec in (0, 1, 2):
            for copy in frame_copies(sec, step):
                copy.start()
                if not (sec == 0 and step == 0):
                    sent.append(copy)
    pot_copy.wait_recv()

    low_lane = lax.broadcasted_iota(jnp.int32, (members * COMP, 128), 1)
    func = lax.rem(lax.broadcasted_iota(jnp.int32, (members * COMP, 128), 0), per)
    outer = (low_lane < CY) | (low_lane >= 128 - CY)
    keep = outer == (func < per // 2)

    for sec in range(3):
        slot, shift, count = slots[sec], shifts[sec], counts[sec]
        for step in range(groups):
            g = lax.rem(me + step, groups)
            for dst, recv in ((got, recv_main), (got_halo, recv_halo)):
                target = dst.at[slot, g, pl.ds(shift, count)]
                pltpu.make_async_copy(target, target, recv.at[sec, g]).wait()

        @pl.loop(0, depth + 2)
        def _(j):
            x = got[slot, :, j].reshape(members * COMP, seg)
            turned = jnp.dot(
                order_ref[: members * COMP], x, preferred_element_type=jnp.float32
            ).astype(jnp.bfloat16)
            orb[slot, j] = turned.reshape(COMP, members, seg)

        @pl.loop(0, depth)
        def _(z):
            x = got[slot, :, z + 1].reshape(members * COMP, seg)
            fine = jnp.dot(
                order_ref[members * COMP :], x, preferred_element_type=jnp.float32
            ).reshape(COMP, members, seg)
            hx = got_halo[slot, :, z + 1].reshape(members * COMP // 2, 128)
            edge = jnp.dot(pick_ref[...], hx, preferred_element_type=jnp.float32)
            edge = jnp.where(keep, edge, 0.0).astype(jnp.bfloat16)
            here = orb[slot, z + 1].reshape(members * COMP, seg)
            term = jnp.dot(here, lap_ref[:seg], preferred_element_type=jnp.float32)
            term += jnp.dot(edge, lap_ref[seg:], preferred_element_type=jnp.float32)
            term = term.reshape(COMP, members, seg)
            pot = got_pot[z].astype(jnp.float32)
            vals = [fine[k] * pot[k : k + 1] for k in range(COMP)]
            width = 1
            while width < COMP:
                vals = [
                    vals[k] + vals[k + width] if not k & width else vals[k - width] - vals[k]
                    for k in range(COMP)
                ]
                width *= 2
            inside = mask_ref[slot, z]
            inside = jnp.concatenate([inside] * (seg // 128), 1) > 0.5
            for c in range(COMP):
                beside = orb[slot, z, c].astype(jnp.float32) + orb[slot, z + 2, c].astype(
                    jnp.float32
                )
                total = term[c] - 0.5 * beside + vals[c] * (1.0 / COMP)
                app[slot, z, c] = jnp.where(inside, total, 0.0).astype(jnp.bfloat16)

    def gram(z, acc):
        for c in range(COMP):
            columns = jnp.concatenate([orb[k, z + 1, c] for k in range(3)], 0)
            images = jnp.concatenate([app[k, z, c] for k in range(3)], 0)
            acc += lax.dot_general(
                jnp.concatenate([columns, images], 0),
                columns,
                (((1,), (1,)), ((), ())),
                preferred_element_type=jnp.float32,
            )
        return acc

    wide = 3 * members
    acc = lax.fori_loop(0, depth, gram, jnp.zeros((2 * wide, wide), jnp.float32))
    rows[...] = jnp.zeros_like(rows)
    for slot in range(3):
        for g in range(groups):
            first = slot * members + g * per
            rows[slot, g, 0:per, 0:wide] = acc[first : first + per]
            rows[slot, g, per : 2 * per, 0:wide] = acc[wide + first : wide + first + per]

    for step in range(groups):
        for sec in (2, 1, 0):
            to = lax.rem(me + step, groups)
            slot = slots[sec]
            source, target = rows.at[slot, to], got_rows.at[slot, me]
            if sec == 0 and step == 0:
                copy = pltpu.make_async_copy(source, target, recv_rows.at[sec, me])
            else:
                copy = pltpu.make_async_remote_copy(
                    src_ref=source,
                    dst_ref=target,
                    send_sem=send_rows.at[sec, step],
                    recv_sem=recv_rows.at[sec, me],
                    device_id=(rows_to[sec], to),
                    device_id_type=MESH,
                )
                sent.append(copy)
            copy.start()
    for sec in range(3):
        for step in range(groups):
            g = lax.rem(me + step, groups)
            target = got_rows.at[slots[sec], g]
            pltpu.make_async_copy(target, target, recv_rows.at[sec, g]).wait()
    parts = []
    for slot in range(3):
        part = got_rows[slot, 0]
        for g in range(1, groups):
            part = part + got_rows[slot, g]
        parts.append(part)
    band = pltpu.roll(parts[0], 2 * members, 1) + pltpu.roll(parts[1], members, 1) + parts[2]
    margin_ref[...] = band[0:per, : margin_ref.shape[1]]
    ham_ref[...] = band[per : 2 * per, : ham_ref.shape[1]]
    pot_copy.wait_send()
    for copy in sent:
        copy.wait_send()


def local(slabs, groups, potential, coefficients, box_center, box_extent):
    slab = lax.axis_index("slab")
    me = lax.axis_index("grp")
    per, box, comp, cells = coefficients.shape
    depth = potential.shape[0]
    members = groups * per
    seg = cells // groups
    odd = slab % 2
    low, up = -depth, depth - 1
    bases = jnp.stack(
        [jnp.where(odd == 1, low, up), jnp.full((), -1, jnp.int32), jnp.where(odd == 1, up, low)]
    ).astype(jnp.int32)
    first = (slab * groups + me) * per
    extents = lax.dynamic_slice_in_dim(box_extent, first, per)
    centers = lax.dynamic_slice_in_dim(box_center, first, per)
    scal = jnp.concatenate([bases, centers - slab * depth - extents // 2, extents])
    vmem = pl.BlockSpec(memory_space=pltpu.VMEM)
    anywhere = pl.BlockSpec(memory_space=pl.ANY)
    main_shape = (3, groups, depth + 2, per * comp, seg)
    halo_shape = (3, groups, depth + 2, per * comp // 2, 128)
    main, halo = pl.pallas_call(
        functools.partial(frame_kernel, groups, depth),
        out_shape=(
            jax.ShapeDtypeStruct(main_shape, jnp.bfloat16),
            jax.ShapeDtypeStruct(halo_shape, jnp.bfloat16),
        ),
        in_specs=[pl.BlockSpec(memory_space=pltpu.SMEM), vmem],
        out_specs=(vmem, vmem),
        name="frames",
    )(scal, coefficients)

    owned = slab + 1 - 2 * odd
    home = (owned + jnp.arange(-1, 2) + slabs) % slabs
    ids = home[:, None] * members + jnp.arange(members)[None, :]
    begin = (
        jnp.take(box_center, ids)
        - home[:, None] * depth
        - jnp.take(box_extent, ids) // 2
        + (jnp.arange(-1, 2) * depth)[:, None]
    )
    at = jnp.arange(depth)[None, :, None] - begin[:, None, :]
    inside = (at >= 0) & (at < jnp.take(box_extent, ids)[:, None, :])
    mask = jnp.broadcast_to(
        inside.astype(jnp.float32)[..., None], (3, depth, members, 128)
    )
    order, pick, lap = matrices(members, per, seg)
    out = jax.ShapeDtypeStruct((per, 5 * members), jnp.float32)
    dma = pltpu.SemaphoreType.DMA
    return pl.pallas_call(
        functools.partial(band_kernel, slabs, groups, depth, per, seg),
        out_shape=(out, out),
        in_specs=[anywhere, anywhere, anywhere, vmem, vmem, vmem, vmem],
        out_specs=(vmem, vmem),
        scratch_shapes=[
            pltpu.VMEM(main_shape, jnp.bfloat16),
            pltpu.VMEM(halo_shape, jnp.bfloat16),
            pltpu.VMEM((depth, comp, seg), jnp.bfloat16),
            pltpu.VMEM((3, depth + 2, comp, members, seg), jnp.bfloat16),
            pltpu.VMEM((3, depth, comp, members, seg), jnp.bfloat16),
            pltpu.VMEM((3, groups, 2 * per, 128), jnp.float32),
            pltpu.VMEM((3, groups, 2 * per, 128), jnp.float32),
            dma((3, groups)),
            dma((3, groups)),
            dma,
            dma((3, groups)),
            dma((3, groups)),
            dma((3, groups)),
            dma,
            dma((3, groups)),
        ],
        compiler_params=pltpu.CompilerParams(collective_id=0, has_side_effects=True),
        name="band",
    )(main, halo, potential, mask, order, pick, lap)


def solution(mesh):
    return jax.shard_map(
        functools.partial(local, mesh.shape["slab"], mesh.shape["grp"]),
        mesh=mesh,
        in_specs=(P("slab", None, None), P(("slab", "grp"), None, None, None), P(), P()),
        out_specs=(P(("slab", "grp"), None), P(("slab", "grp"), None)),
        check_vma=False,
    )
```

```python
import functools

import jax
import jax.numpy as jnp
import numpy as np
from jax import lax
from jax.experimental import pallas as pl
from jax.experimental.pallas import tpu as pltpu
from jax.sharding import PartitionSpec as P

COMP = 8
CX = 32
CY = 32
MESH = pl.DeviceIdType.MESH


def haar_signs():
    ids = np.arange(COMP)
    common = ids[:, None] & ids[None, :]
    parity = (common % 2 + common // 2 % 2 + common // 4 % 2) % 2
    return (1 - 2 * parity).astype(np.float32)


def matrices(members, per, seg):
    rows = members * COMP
    order = np.zeros((COMP, members, members, COMP), np.float32)
    haar = np.zeros((COMP, members, members, COMP), np.float32)
    signs = haar_signs()
    half = per // 2
    pick = np.zeros((COMP, members, members // 2, COMP), np.float32)
    for n in range(members):
        group, func = divmod(n, per)
        for c in range(COMP):
            order[c, n, n, c] = 1.0
            haar[c, n, n, :] = signs[c]
            pick[c, n, group * half + func % half, c] = 1.0
    stacked = np.concatenate([order.reshape(rows, rows), haar.reshape(rows, rows)], 0)
    lap = np.zeros((seg + 128, seg), np.float32)
    for i in range(seg):
        lap[i, i] = 3.0
        if i % CY:
            lap[i - 1, i] = -0.5
            lap[i, i - 1] = -0.5
        if i >= CY:
            lap[i - CY, i] = -0.5
            lap[i, i - CY] = -0.5
    for i in range(CY):
        lap[seg + 128 - CY + i, i] = -0.5
        lap[seg + 64 - CY + i, i] = -0.5
        lap[seg + i, seg - CY + i] = -0.5
        lap[seg + 64 + i, seg - CY + i] = -0.5
    as_bf16 = lambda value: jnp.asarray(value, jnp.bfloat16)
    return as_bf16(stacked), as_bf16(pick.reshape(rows, -1)), as_bf16(lap)


def band_kernel(
    slabs,
    groups,
    depth,
    coef_ref,
    pot_ref,
    center_ref,
    extent_ref,
    order_ref,
    pick_ref,
    lap_ref,
    out_ref,
    main,
    halo,
    got,
    got_halo,
    got_pot,
    orb,
    app,
    limits,
    rows,
    got_rows,
    send_main,
    send_halo,
    send_pot,
    send_rows,
    recv_main,
    recv_halo,
    recv_pot,
    recv_rows,
):
    slab = lax.axis_index("slab")
    me = lax.axis_index("grp")
    per, box, comp, cells = coef_ref.shape
    seg = cells // groups
    half = per // 2
    members = groups * per
    odd = lax.rem(slab, 2)
    partner = slab + 1 - 2 * odd
    ahead = lax.rem(slab + 2, slabs)
    behind = lax.rem(slab + slabs - 2, slabs)
    is_odd = odd == 1
    frame_to = [lax.select(is_odd, ahead, slab), partner, lax.select(is_odd, slab, behind)]
    rows_to = [lax.select(is_odd, behind, slab), partner, lax.select(is_odd, slab, ahead)]
    bases = [depth - 1, -1, -depth]
    counts = [depth, depth + 2, depth + 1]
    offsets = [0, 0, 1]
    halo_counts = [depth - 1, depth, depth]
    halo_from = [1, 1, 0]
    if groups == 4:
        targets = [lax.rem(me + 2, groups), 3 - me, me + 1 - 2 * lax.rem(me, 2), me]
    else:
        targets = [lax.rem(me + 1 + step, groups) for step in range(groups)]

    barrier = pltpu.get_barrier_semaphore()
    for to in targets:
        for place in (slab, partner, ahead, behind):
            if place is slab and to is targets[-1]:
                continue
            pl.semaphore_signal(barrier, inc=1, device_id=(place, to), device_id_type=MESH)

    @pl.loop(0, groups)
    def _(g):
        plane = jnp.zeros(got.shape[3:], got.dtype)
        got[0, g, depth] = plane
        got[0, g, depth + 1] = plane
        got[2, g, 0] = plane
        got_halo[0, g, depth - 1] = jnp.zeros(got_halo.shape[3:], got_halo.dtype)

    lane = lax.broadcasted_iota(jnp.int32, (comp, 128), 1)
    first = (slab * groups + me) * per
    extents = [extent_ref[first + f] for f in range(per)]
    starts = [
        center_ref[first + f] - slab * depth - lax.shift_right_logical(extents[f], 1)
        for f in range(per)
    ]

    def build(slot, j, with_halo):
        planes = []
        for f in range(per):
            p = bases[slot] + j - starts[f]
            inside = (p >= 0) & (p < extents[f])
            value = coef_ref[f, jnp.clip(p, 0, box - 1)].astype(jnp.float32)
            planes.append(jnp.where(inside, value, 0.0))
        for g in range(groups):
            at = slice(g * seg, (g + 1) * seg)
            main[slot, g, j] = jnp.concatenate([v[:, at] for v in planes], 0).astype(
                jnp.bfloat16
            )
            if not with_halo:
                continue
            tiles = []
            for v in planes:
                zero = jnp.zeros((comp, 128), jnp.float32)
                before = v[:, g * seg - 128 : g * seg] if g else zero
                after = v[:, (g + 1) * seg : (g + 1) * seg + 128] if g < groups - 1 else zero
                tiles.append(
                    jnp.where(lane >= 128 - CY, before, jnp.where(lane < CY, after, 0.0))
                )
            packed = [tiles[f] + pltpu.roll(tiles[half + f], 64, 1) for f in range(half)]
            halo[slot, g, j - halo_from[slot]] = jnp.concatenate(packed, 0).astype(jnp.bfloat16)

    def build_slot(slot):
        low, high = halo_from[slot], halo_from[slot] + halo_counts[slot]

        @pl.loop(low, high)
        def _(j):
            build(slot, j, True)

        for j in (*range(low), *range(high, counts[slot])):
            build(slot, j, False)

    self_slot = {0: jnp.logical_not(is_odd), 2: is_odd}
    unsent = []

    def move(slot, step, source, target, send, recv, to_slab):
        remote = pltpu.make_async_remote_copy(
            src_ref=source,
            dst_ref=target,
            send_sem=send.at[slot, step],
            recv_sem=recv.at[slot, me],
            device_id=(to_slab, targets[step]),
            device_id_type=MESH,
        )
        if slot == 1 or step < groups - 1:
            remote.start()
            unsent.append((None, remote))
            return
        here = self_slot[slot]

        @pl.when(here)
        def _():
            pltpu.make_async_copy(source, target, recv.at[slot, me]).start()

        @pl.when(jnp.logical_not(here))
        def _():
            remote.start()

        unsent.append((jnp.logical_not(here), remote))

    def send_slot(slot):
        for step, to in enumerate(targets):
            move(
                slot,
                step,
                main.at[slot, to, pl.ds(0, counts[slot])],
                got.at[slot, me, pl.ds(offsets[slot], counts[slot])],
                send_main,
                recv_main,
                frame_to[slot],
            )
            move(
                slot,
                step,
                halo.at[slot, to, pl.ds(0, halo_counts[slot])],
                got_halo.at[slot, me, pl.ds(0, halo_counts[slot])],
                send_halo,
                recv_halo,
                frame_to[slot],
            )

    pot_copy = pltpu.make_async_remote_copy(
        src_ref=pot_ref.at[:, :, pl.ds(pl.multiple_of(me * seg, seg), seg)],
        dst_ref=got_pot,
        send_sem=send_pot,
        recv_sem=recv_pot,
        device_id=(partner, me),
        device_id_type=MESH,
    )

    turn = (1, 0, 2)
    build_slot(turn[0])
    pl.semaphore_wait(barrier, 4 * groups - 1)
    build_slot(turn[1])
    send_slot(turn[0])
    pot_copy.start()
    build_slot(turn[2])
    send_slot(turn[1])

    member = lax.broadcasted_iota(jnp.int32, (members, seg), 0)
    for slot in range(3):
        home = lax.rem(partner + slot - 1 + slabs, slabs)
        begin = jnp.zeros((members, seg), jnp.int32)
        end = jnp.zeros((members, seg), jnp.int32)
        for n in range(members):
            extent = extent_ref[home * members + n]
            start = (
                center_ref[home * members + n]
                - home * depth
                - lax.shift_right_logical(extent, 1)
                + (slot - 1) * depth
            )
            begin = jnp.where(member == n, start, begin)
            end = jnp.where(member == n, start + extent, end)
        limits[slot, 0] = begin
        limits[slot, 1] = end

    send_slot(turn[2])
    pot_copy.wait_recv()

    at_lane = lax.broadcasted_iota(jnp.int32, (members * COMP, 128), 1)
    func = lax.rem(lax.broadcasted_iota(jnp.int32, (members * COMP, 128), 0), per)
    keep = ((at_lane < CY) | (at_lane >= 128 - CY)) == (func < half)

    for slot in turn:
        for g in targets[::-1]:
            for dst, recv, offset, count in (
                (got, recv_main, offsets[slot], counts[slot]),
                (got_halo, recv_halo, 0, halo_counts[slot]),
            ):
                target = dst.at[slot, g, pl.ds(offset, count)]
                pltpu.make_async_copy(target, target, recv.at[slot, g]).wait()

        @pl.loop(0, depth + 2, unroll=(depth + 2) // 2)
        def _(j):
            x = got[slot, :, j].reshape(members * COMP, seg)
            turned = jnp.dot(
                order_ref[: members * COMP], x, preferred_element_type=jnp.float32
            ).astype(jnp.bfloat16)
            orb[slot, j] = turned.reshape(COMP, members, seg)

        @pl.loop(0, depth, unroll=4)
        def _(z):
            x = got[slot, :, z + 1].reshape(members * COMP, seg)
            fine = jnp.dot(
                order_ref[members * COMP :], x, preferred_element_type=jnp.float32
            ).reshape(COMP, members, seg)
            hx = got_halo[slot, :, z].reshape(members * COMP // 2, 128)
            edge = jnp.dot(pick_ref[...], hx, preferred_element_type=jnp.float32)
            edge = jnp.where(keep, edge, 0.0).astype(jnp.bfloat16)
            here = orb[slot, z + 1].reshape(members * COMP, seg)
            term = jnp.dot(here, lap_ref[:seg], preferred_element_type=jnp.float32)
            term += jnp.dot(edge, lap_ref[seg:], preferred_element_type=jnp.float32)
            term = term.reshape(COMP, members, seg)
            pot = got_pot[z].astype(jnp.float32)
            vals = [fine[k] * pot[k : k + 1] for k in range(COMP)]
            width = 1
            while width < COMP:
                vals = [
                    vals[k] + vals[k + width] if not k & width else vals[k - width] - vals[k]
                    for k in range(COMP)
                ]
                width *= 2
            inside = (limits[slot, 0] <= z) & (limits[slot, 1] > z)
            for c in range(COMP):
                beside = orb[slot, z, c].astype(jnp.float32) + orb[slot, z + 2, c].astype(
                    jnp.float32
                )
                total = term[c] - 0.5 * beside + vals[c] * (1.0 / COMP)
                app[slot, z, c] = jnp.where(inside, total, 0.0).astype(jnp.bfloat16)

    def gram(z, acc):
        for c in range(COMP):
            columns = jnp.concatenate([orb[k, z + 1, c] for k in range(3)], 0)
            images = jnp.concatenate([app[k, z, c] for k in range(3)], 0)
            acc += lax.dot_general(
                jnp.concatenate([columns, images], 0),
                columns,
                (((1,), (1,)), ((), ())),
                preferred_element_type=jnp.float32,
            )
        return acc

    wide = 3 * members
    rows[...] = jnp.zeros_like(rows)
    acc = lax.fori_loop(0, depth, gram, jnp.zeros((2 * wide, wide), jnp.float32))
    for slot in range(3):
        for g in range(groups):
            at = slot * members + g * per
            rows[slot, g, 0:per, 0:wide] = acc[at : at + per]
            rows[slot, g, per : 2 * per, 0:wide] = acc[wide + at : wide + at + per]

    for step, to in enumerate(targets):
        for slot in (1, 0, 2):
            move(
                slot,
                step,
                rows.at[slot, to],
                got_rows.at[slot, me],
                send_rows,
                recv_rows,
                rows_to[slot],
            )
    for slot in range(3):
        for g in range(groups):
            target = got_rows.at[slot, g]
            pltpu.make_async_copy(target, target, recv_rows.at[slot, g]).wait()
    parts = []
    for slot in range(3):
        part = got_rows[slot, 0]
        for g in range(1, groups):
            part = part + got_rows[slot, g]
        parts.append(part)
    out_ref[...] = (
        pltpu.roll(parts[0], 2 * members, 1) + pltpu.roll(parts[1], members, 1) + parts[2]
    )
    pot_copy.wait_send()
    for condition, copy in unsent:
        if condition is None:
            copy.wait_send()
        else:
            pl.when(condition)(copy.wait_send)


def split_kernel(band_ref, margin_ref, ham_ref):
    per, width = margin_ref.shape
    margin_ref[...] = band_ref[:per, :width]
    ham_ref[...] = band_ref[per:, :width]


def local(slabs, groups, potential, coefficients, box_center, box_extent):
    per, box, comp, cells = coefficients.shape
    depth = potential.shape[0]
    members = groups * per
    seg = cells // groups
    vmem = pl.BlockSpec(memory_space=pltpu.VMEM)
    smem = pl.BlockSpec(memory_space=pltpu.SMEM)
    anywhere = pl.BlockSpec(memory_space=pl.ANY)
    frames = pltpu.VMEM((3, groups, depth + 2, per * comp, seg), jnp.bfloat16)
    halos = pltpu.VMEM((3, groups, depth, per * comp // 2, 128), jnp.bfloat16)
    sums = pltpu.VMEM((3, groups, 2 * per, 128), jnp.float32)
    dma = pltpu.SemaphoreType.DMA
    band = pl.pallas_call(
        functools.partial(band_kernel, slabs, groups, depth),
        out_shape=jax.ShapeDtypeStruct((2 * per, 128), jnp.float32),
        in_specs=[vmem, anywhere, smem, smem, vmem, vmem, vmem],
        out_specs=vmem,
        scratch_shapes=[
            frames,
            halos,
            frames,
            halos,
            pltpu.VMEM((depth, comp, seg), jnp.bfloat16),
            pltpu.VMEM((3, depth + 2, comp, members, seg), jnp.bfloat16),
            pltpu.VMEM((3, depth, comp, members, seg), jnp.bfloat16),
            pltpu.VMEM((3, 2, members, seg), jnp.int32),
            sums,
            sums,
            dma((3, groups)),
            dma((3, groups)),
            dma,
            dma((3, groups)),
            dma((3, groups)),
            dma((3, groups)),
            dma,
            dma((3, groups)),
        ],
        compiler_params=pltpu.CompilerParams(collective_id=0, has_side_effects=True),
        name="band",
    )(coefficients, potential, box_center, box_extent, *matrices(members, per, seg))
    out = jax.ShapeDtypeStruct((per, 5 * members), jnp.float32)
    return pl.pallas_call(
        split_kernel, out_shape=(out, out), in_specs=[vmem], out_specs=(vmem, vmem), name="split"
    )(band)


def solution(mesh):
    return jax.shard_map(
        functools.partial(local, mesh.shape["slab"], mesh.shape["grp"]),
        mesh=mesh,
        in_specs=(P("slab", None, None), P(("slab", "grp"), None, None, None), P(), P()),
        out_specs=(P(("slab", "grp"), None), P(("slab", "grp"), None)),
        check_vma=False,
    )
```

```python
import functools

import jax
import jax.numpy as jnp
import numpy as np
from jax import lax
from jax.experimental import pallas as pl
from jax.experimental.pallas import tpu as pltpu
from jax.sharding import PartitionSpec as P

COMP = 8
CX = 32
CY = 32
MESH = pl.DeviceIdType.MESH


def haar_signs():
    ids = np.arange(COMP)
    common = ids[:, None] & ids[None, :]
    parity = (common % 2 + common // 2 % 2 + common // 4 % 2) % 2
    return (1 - 2 * parity).astype(np.float32)


def matrices(members, per, seg):
    rows = members * COMP
    order = np.zeros((COMP, members, members, COMP), np.float32)
    haar = np.zeros((COMP, members, members, COMP), np.float32)
    signs = haar_signs()
    half = per // 2
    pick = np.zeros((COMP, members, members // 2, COMP), np.float32)
    for n in range(members):
        group, func = divmod(n, per)
        for c in range(COMP):
            order[c, n, n, c] = 1.0
            haar[c, n, n, :] = signs[c]
            pick[c, n, group * half + func % half, c] = 1.0
    stacked = np.concatenate([order.reshape(rows, rows), haar.reshape(rows, rows)], 0)
    lap = np.zeros((seg + 128, seg), np.float32)
    for i in range(seg):
        lap[i, i] = 3.0
        if i % CY:
            lap[i - 1, i] = -0.5
            lap[i, i - 1] = -0.5
        if i >= CY:
            lap[i - CY, i] = -0.5
            lap[i, i - CY] = -0.5
    for i in range(CY):
        lap[seg + 128 - CY + i, i] = -0.5
        lap[seg + 64 - CY + i, i] = -0.5
        lap[seg + i, seg - CY + i] = -0.5
        lap[seg + 64 + i, seg - CY + i] = -0.5
    as_bf16 = lambda value: jnp.asarray(value, jnp.bfloat16)
    return as_bf16(stacked), as_bf16(pick.reshape(rows, -1)), as_bf16(lap)


def band_kernel(
    slabs,
    groups,
    depth,
    coef_ref,
    pot_ref,
    center_ref,
    extent_ref,
    order_ref,
    pick_ref,
    lap_ref,
    out_ref,
    main,
    halo,
    got,
    got_halo,
    got_pot,
    orb,
    app,
    limits,
    rows,
    got_rows,
    send_main,
    send_halo,
    send_pot,
    send_rows,
    recv_main,
    recv_halo,
    recv_pot,
    recv_rows,
):
    slab = lax.axis_index("slab")
    me = lax.axis_index("grp")
    per, box, comp, cells = coef_ref.shape
    seg = cells // groups
    half = per // 2
    members = groups * per
    odd = lax.rem(slab, 2)
    partner = slab + 1 - 2 * odd
    ahead = lax.rem(slab + 2, slabs)
    behind = lax.rem(slab + slabs - 2, slabs)
    is_odd = odd == 1
    slots = [2 * odd, 1, 2 - 2 * odd]
    frame_to = [slab, partner, lax.select(is_odd, ahead, behind)]
    rows_to = [slab, partner, lax.select(is_odd, behind, ahead)]
    relayed = (0, 1) if groups == 4 else ()
    direct = tuple(step for step in range(groups) if step not in relayed)
    if groups == 4:
        targets = [lax.rem(me + 2, groups), 3 - me, me + 1 - 2 * lax.rem(me, 2), me]
    else:
        targets = [lax.rem(me + 1 + step, groups) for step in range(groups)]

    barrier = pltpu.get_barrier_semaphore()
    for to in targets:
        for place in (slab, partner, ahead, behind):
            if place is slab and to is targets[-1]:
                continue
            pl.semaphore_signal(barrier, inc=1, device_id=(place, to), device_id_type=MESH)

    lane = lax.broadcasted_iota(jnp.int32, (comp, 128), 1)
    first = (slab * groups + me) * per
    extents = [extent_ref[first + f] for f in range(per)]
    starts = [
        center_ref[first + f] - slab * depth - lax.shift_right_logical(extents[f], 1)
        for f in range(per)
    ]

    def build(kind, j, with_halo):
        planes = []
        for f in range(per):
            p = j - 1 - starts[f]
            if kind == 0:
                p = p + depth
                p = jnp.where(p < extents[f], p, p - 2 * depth)
            inside = (p >= 0) & (p < extents[f])
            value = coef_ref[f, jnp.clip(p, 0, box - 1)].astype(jnp.float32)
            planes.append(jnp.where(inside, value, 0.0))
        for g in range(groups):
            at = slice(g * seg, (g + 1) * seg)
            main[kind, g, j] = jnp.concatenate([v[:, at] for v in planes], 0).astype(
                jnp.bfloat16
            )
            if not with_halo:
                continue
            tiles = []
            for v in planes:
                zero = jnp.zeros((comp, 128), jnp.float32)
                before = v[:, g * seg - 128 : g * seg] if g else zero
                after = v[:, (g + 1) * seg : (g + 1) * seg + 128] if g < groups - 1 else zero
                tiles.append(
                    jnp.where(lane >= 128 - CY, before, jnp.where(lane < CY, after, 0.0))
                )
            packed = [tiles[f] + pltpu.roll(tiles[half + f], 64, 1) for f in range(half)]
            halo[kind, g, j - 1] = jnp.concatenate(packed, 0).astype(jnp.bfloat16)

    def build_set(kind):
        @pl.loop(1, depth + 1)
        def _(j):
            build(kind, j, True)

        build(kind, 0, False)
        build(kind, depth + 1, False)

    unsent = []

    def move(role, step, source, target, send, recv, to):
        if role == 0 and step == groups - 1:
            pltpu.make_async_copy(source, target, recv).start()
            return
        copy = pltpu.make_async_remote_copy(
            src_ref=source,
            dst_ref=target,
            send_sem=send.at[role, step],
            recv_sem=recv,
            device_id=to,
            device_id_type=MESH,
        )
        copy.start()
        unsent.append(copy)

    def send(role, step):
        to, kind = targets[step], role % 2
        for source, target, sem, recv in (
            (main, got, send_main, recv_main),
            (halo, got_halo, send_halo, recv_halo),
        ):
            move(
                role,
                step,
                source.at[kind, to],
                target.at[role, me],
                sem,
                recv.at[role, me],
                (frame_to[role], to),
            )

    def arrived(role, g):
        for target, recv in ((got, recv_main), (got_halo, recv_halo)):
            block = target.at[role, g]
            pltpu.make_async_copy(block, block, recv.at[role, g]).wait()

    def relay(step):
        source = targets[step]
        for block, sem, recv in (
            (got, send_main, recv_main),
            (got_halo, send_halo, recv_halo),
        ):
            move(
                2,
                step,
                block.at[0, source],
                block.at[2, source],
                sem,
                recv.at[2, source],
                (frame_to[2], me),
            )

    pot_copy = pltpu.make_async_remote_copy(
        src_ref=pot_ref.at[:, :, pl.ds(pl.multiple_of(me * seg, seg), seg)],
        dst_ref=got_pot,
        send_sem=send_pot,
        recv_sem=recv_pot,
        device_id=(partner, me),
        device_id_type=MESH,
    )

    build_set(0)
    pl.semaphore_wait(barrier, 4 * groups - 1)
    build_set(1)
    for step in relayed:
        send(0, step)
    for step in direct:
        send(2, step)
    for step in direct:
        send(0, step)
    pot_copy.start()

    member = lax.broadcasted_iota(jnp.int32, (members, seg), 0)
    for slot in range(3):
        home = lax.rem(partner + slot - 1 + slabs, slabs)
        begin = jnp.zeros((members, seg), jnp.int32)
        end = jnp.zeros((members, seg), jnp.int32)
        for n in range(members):
            extent = extent_ref[home * members + n]
            start = (
                center_ref[home * members + n]
                - home * depth
                - lax.shift_right_logical(extent, 1)
                + (slot - 1) * depth
            )
            begin = jnp.where(member == n, start, begin)
            end = jnp.where(member == n, start + extent, end)
        limits[slot, 0] = begin
        limits[slot, 1] = end

    for step in (*direct, *relayed):
        send(1, step)
    for step in relayed:
        arrived(0, targets[step])
        relay(step)
    pot_copy.wait_recv()

    at_lane = lax.broadcasted_iota(jnp.int32, (members * COMP, 128), 1)
    func = lax.rem(lax.broadcasted_iota(jnp.int32, (members * COMP, 128), 0), per)
    keep = ((at_lane < CY) | (at_lane >= 128 - CY)) == (func < half)

    for role in range(3):
        slot = slots[role]
        for step in direct if role == 0 else range(groups):
            arrived(role, targets[step])

        @pl.loop(0, depth + 2, unroll=(depth + 2) // 2)
        def _(j):
            x = got[role, :, j].reshape(members * COMP, seg)
            turned = jnp.dot(
                order_ref[: members * COMP], x, preferred_element_type=jnp.float32
            ).reshape(COMP, members, seg)
            if role != 1:
                inside = (limits[slot, 0] < j) & (limits[slot, 1] >= j)
                turned = jnp.where(inside[None], turned, 0.0)
            orb[slot, j] = turned.astype(jnp.bfloat16)

        @pl.loop(0, depth, unroll=4)
        def _(z):
            x = got[role, :, z + 1].reshape(members * COMP, seg)
            fine = jnp.dot(
                order_ref[members * COMP :], x, preferred_element_type=jnp.float32
            ).reshape(COMP, members, seg)
            hx = got_halo[role, :, z].reshape(members * COMP // 2, 128)
            edge = jnp.dot(pick_ref[...], hx, preferred_element_type=jnp.float32)
            edge = jnp.where(keep, edge, 0.0).astype(jnp.bfloat16)
            here = orb[slot, z + 1].reshape(members * COMP, seg)
            term = jnp.dot(here, lap_ref[:seg], preferred_element_type=jnp.float32)
            term += jnp.dot(edge, lap_ref[seg:], preferred_element_type=jnp.float32)
            term = term.reshape(COMP, members, seg)
            pot = got_pot[z].astype(jnp.float32)
            vals = [fine[k] * pot[k : k + 1] for k in range(COMP)]
            width = 1
            while width < COMP:
                vals = [
                    vals[k] + vals[k + width] if not k & width else vals[k - width] - vals[k]
                    for k in range(COMP)
                ]
                width *= 2
            inside = (limits[slot, 0] <= z) & (limits[slot, 1] > z)
            for c in range(COMP):
                beside = orb[slot, z, c].astype(jnp.float32) + orb[slot, z + 2, c].astype(
                    jnp.float32
                )
                total = term[c] - 0.5 * beside + vals[c] * (1.0 / COMP)
                app[slot, z, c] = jnp.where(inside, total, 0.0).astype(jnp.bfloat16)

    def gram(z, acc):
        for c in range(COMP):
            columns = jnp.concatenate([orb[k, z + 1, c] for k in range(3)], 0)
            images = jnp.concatenate([app[k, z, c] for k in range(3)], 0)
            acc += lax.dot_general(
                jnp.concatenate([columns, images], 0),
                columns,
                (((1,), (1,)), ((), ())),
                preferred_element_type=jnp.float32,
            )
        return acc

    wide = 3 * members
    rows[...] = jnp.zeros_like(rows)
    acc = lax.fori_loop(0, depth, gram, jnp.zeros((2 * wide, wide), jnp.float32))
    for slot in range(3):
        for g in range(groups):
            at = slot * members + g * per
            rows[slot, g, 0:per, 0:wide] = acc[at : at + per]
            rows[slot, g, per : 2 * per, 0:wide] = acc[wide + at : wide + at + per]

    for step, to in enumerate(targets):
        for role in (2, 1, 0):
            slot = slots[role]
            move(
                role,
                step,
                rows.at[slot, to],
                got_rows.at[slot, me],
                send_rows,
                recv_rows.at[role, me],
                (rows_to[role], to),
            )
    for role in range(3):
        for g in range(groups):
            block = got_rows.at[slots[role], g]
            pltpu.make_async_copy(block, block, recv_rows.at[role, g]).wait()
    parts = []
    for slot in range(3):
        part = got_rows[slot, 0]
        for g in range(1, groups):
            part = part + got_rows[slot, g]
        parts.append(part)
    out_ref[...] = (
        pltpu.roll(parts[0], 2 * members, 1) + pltpu.roll(parts[1], members, 1) + parts[2]
    )
    pot_copy.wait_send()
    for copy in unsent:
        copy.wait_send()


def split_kernel(band_ref, margin_ref, ham_ref):
    per, width = margin_ref.shape
    margin_ref[...] = band_ref[:per, :width]
    ham_ref[...] = band_ref[per:, :width]


def local(slabs, groups, potential, coefficients, box_center, box_extent):
    per, box, comp, cells = coefficients.shape
    depth = potential.shape[0]
    members = groups * per
    seg = cells // groups
    vmem = pl.BlockSpec(memory_space=pltpu.VMEM)
    smem = pl.BlockSpec(memory_space=pltpu.SMEM)
    anywhere = pl.BlockSpec(memory_space=pl.ANY)
    frames = lambda n: pltpu.VMEM((n, groups, depth + 2, per * comp, seg), jnp.bfloat16)
    halos = lambda n: pltpu.VMEM((n, groups, depth, per * comp // 2, 128), jnp.bfloat16)
    sums = pltpu.VMEM((3, groups, 2 * per, 128), jnp.float32)
    dma = pltpu.SemaphoreType.DMA
    band = pl.pallas_call(
        functools.partial(band_kernel, slabs, groups, depth),
        out_shape=jax.ShapeDtypeStruct((2 * per, 128), jnp.float32),
        in_specs=[vmem, anywhere, smem, smem, vmem, vmem, vmem],
        out_specs=vmem,
        scratch_shapes=[
            frames(2),
            halos(2),
            frames(3),
            halos(3),
            pltpu.VMEM((depth, comp, seg), jnp.bfloat16),
            pltpu.VMEM((3, depth + 2, comp, members, seg), jnp.bfloat16),
            pltpu.VMEM((3, depth, comp, members, seg), jnp.bfloat16),
            pltpu.VMEM((3, 2, members, seg), jnp.int32),
            sums,
            sums,
            dma((3, groups)),
            dma((3, groups)),
            dma,
            dma((3, groups)),
            dma((3, groups)),
            dma((3, groups)),
            dma,
            dma((3, groups)),
        ],
        compiler_params=pltpu.CompilerParams(collective_id=0, has_side_effects=True),
        name="band",
    )(coefficients, potential, box_center, box_extent, *matrices(members, per, seg))
    out = jax.ShapeDtypeStruct((per, 5 * members), jnp.float32)
    return pl.pallas_call(
        split_kernel, out_shape=(out, out), in_specs=[vmem], out_specs=(vmem, vmem), name="split"
    )(band)


def solution(mesh):
    return jax.shard_map(
        functools.partial(local, mesh.shape["slab"], mesh.shape["grp"]),
        mesh=mesh,
        in_specs=(P("slab", None, None), P(("slab", "grp"), None, None, None), P(), P()),
        out_specs=(P(("slab", "grp"), None), P(("slab", "grp"), None)),
        check_vma=False,
    )
```

```python
import functools

import jax
import jax.numpy as jnp
import numpy as np
from jax import lax
from jax.experimental import pallas as pl
from jax.experimental.pallas import tpu as pltpu
from jax.sharding import PartitionSpec as P

COMP = 8
CX = 32
CY = 32
MESH = pl.DeviceIdType.MESH


def haar_signs():
    ids = np.arange(COMP)
    common = ids[:, None] & ids[None, :]
    parity = (common % 2 + common // 2 % 2 + common // 4 % 2) % 2
    return (1 - 2 * parity).astype(np.float32)


def matrices(members, per, seg):
    rows = members * COMP
    order = np.zeros((COMP, members, members, COMP), np.float32)
    haar = np.zeros((COMP, members, members, COMP), np.float32)
    signs = haar_signs()
    half = per // 2
    pick = np.zeros((COMP, members, members // 2, COMP), np.float32)
    for n in range(members):
        group, func = divmod(n, per)
        for c in range(COMP):
            order[c, n, n, c] = 1.0
            haar[c, n, n, :] = signs[c]
            pick[c, n, group * half + func % half, c] = 1.0
    stacked = np.concatenate([order.reshape(rows, rows), haar.reshape(rows, rows)], 0)
    lap = np.zeros((seg + 128, seg), np.float32)
    for i in range(seg):
        lap[i, i] = 3.0
        if i % CY:
            lap[i - 1, i] = -0.5
            lap[i, i - 1] = -0.5
        if i >= CY:
            lap[i - CY, i] = -0.5
            lap[i, i - CY] = -0.5
    for i in range(CY):
        lap[seg + 128 - CY + i, i] = -0.5
        lap[seg + 64 - CY + i, i] = -0.5
        lap[seg + i, seg - CY + i] = -0.5
        lap[seg + 64 + i, seg - CY + i] = -0.5
    as_bf16 = lambda value: jnp.asarray(value, jnp.bfloat16)
    return as_bf16(stacked), as_bf16(pick.reshape(rows, -1)), as_bf16(lap)


def band_kernel(
    slabs,
    groups,
    depth,
    coef_ref,
    pot_ref,
    center_ref,
    extent_ref,
    order_ref,
    pick_ref,
    lap_ref,
    out_ref,
    main,
    halo,
    got,
    got_halo,
    got_pot,
    orb,
    app,
    limits,
    rows,
    got_rows,
    send_main,
    send_halo,
    send_pot,
    send_rows,
    recv_main,
    recv_halo,
    recv_pot,
    recv_rows,
):
    slab = lax.axis_index("slab")
    me = lax.axis_index("grp")
    per, box, comp, cells = coef_ref.shape
    seg = cells // groups
    half = per // 2
    members = groups * per
    odd = lax.rem(slab, 2)
    partner = slab + 1 - 2 * odd
    ahead = lax.rem(slab + 2, slabs)
    behind = lax.rem(slab + slabs - 2, slabs)
    is_odd = odd == 1
    slots = [2 * odd, 1, 2 - 2 * odd]
    frame_to = [slab, partner, lax.select(is_odd, ahead, behind)]
    rows_to = [slab, partner, lax.select(is_odd, behind, ahead)]
    relayed = (0, 1) if groups == 4 else ()
    direct = tuple(step for step in range(groups) if step not in relayed)
    if groups == 4:
        targets = [lax.rem(me + 2, groups), 3 - me, me + 1 - 2 * lax.rem(me, 2), me]
    else:
        targets = [lax.rem(me + 1 + step, groups) for step in range(groups)]

    barrier = pltpu.get_barrier_semaphore()
    for to in targets:
        for place in (slab, partner, ahead, behind):
            if place is slab and to is targets[-1]:
                continue
            pl.semaphore_signal(barrier, inc=1, device_id=(place, to), device_id_type=MESH)

    lane = lax.broadcasted_iota(jnp.int32, (comp, 128), 1)
    first = (slab * groups + me) * per
    extents = [extent_ref[first + f] for f in range(per)]
    starts = [
        center_ref[first + f] - slab * depth - lax.shift_right_logical(extents[f], 1)
        for f in range(per)
    ]

    def build(kind, j, with_halo):
        planes = []
        for f in range(per):
            p = j - 1 - starts[f]
            if kind == 0:
                p = p + depth
                p = jnp.where(p < extents[f], p, p - 2 * depth)
            inside = (p >= 0) & (p < extents[f])
            value = coef_ref[f, jnp.clip(p, 0, box - 1)].astype(jnp.float32)
            planes.append(jnp.where(inside, value, 0.0))
        for g in range(groups):
            at = slice(g * seg, (g + 1) * seg)
            main[kind, g, j] = jnp.concatenate([v[:, at] for v in planes], 0).astype(
                jnp.bfloat16
            )
            if not with_halo:
                continue
            tiles = []
            for v in planes:
                zero = jnp.zeros((comp, 128), jnp.float32)
                before = v[:, g * seg - 128 : g * seg] if g else zero
                after = v[:, (g + 1) * seg : (g + 1) * seg + 128] if g < groups - 1 else zero
                tiles.append(
                    jnp.where(lane >= 128 - CY, before, jnp.where(lane < CY, after, 0.0))
                )
            packed = [tiles[f] + pltpu.roll(tiles[half + f], 64, 1) for f in range(half)]
            halo[kind, g, j - 1] = jnp.concatenate(packed, 0).astype(jnp.bfloat16)

    def build_set(kind):
        @pl.loop(1, depth + 1)
        def _(j):
            build(kind, j, True)

        build(kind, 0, False)
        build(kind, depth + 1, False)

    unsent = []

    def move(role, step, source, target, send, recv, to):
        if role == 0 and step == groups - 1:
            pltpu.make_async_copy(source, target, recv).start()
            return
        copy = pltpu.make_async_remote_copy(
            src_ref=source,
            dst_ref=target,
            send_sem=send.at[role, step],
            recv_sem=recv,
            device_id=to,
            device_id_type=MESH,
        )
        copy.start()
        unsent.append(copy)

    def send(role, step):
        to, kind = targets[step], role % 2
        for source, target, sem, recv in (
            (main, got, send_main, recv_main),
            (halo, got_halo, send_halo, recv_halo),
        ):
            move(
                role,
                step,
                source.at[kind, to],
                target.at[role, me],
                sem,
                recv.at[role, me],
                (frame_to[role], to),
            )

    def arrived(role, g):
        for target, recv in ((got, recv_main), (got_halo, recv_halo)):
            block = target.at[role, g]
            pltpu.make_async_copy(block, block, recv.at[role, g]).wait()

    def relay(step):
        source = targets[step]
        for block, sem, recv in (
            (got, send_main, recv_main),
            (got_halo, send_halo, recv_halo),
        ):
            move(
                2,
                step,
                block.at[0, source],
                block.at[2, source],
                sem,
                recv.at[2, source],
                (frame_to[2], me),
            )

    pot_copy = pltpu.make_async_remote_copy(
        src_ref=pot_ref.at[:, :, pl.ds(pl.multiple_of(me * seg, seg), seg)],
        dst_ref=got_pot,
        send_sem=send_pot,
        recv_sem=recv_pot,
        device_id=(partner, me),
        device_id_type=MESH,
    )

    build_set(0)
    pl.semaphore_wait(barrier, 4 * groups - 1)
    build_set(1)
    for step in relayed:
        send(0, step)
    for step in direct:
        send(2, step)
    for step in direct:
        send(0, step)
    pot_copy.start()

    member = lax.broadcasted_iota(jnp.int32, (members, seg), 0)
    for slot in range(3):
        home = lax.rem(partner + slot - 1 + slabs, slabs)
        begin = jnp.zeros((members, seg), jnp.int32)
        end = jnp.zeros((members, seg), jnp.int32)
        for n in range(members):
            extent = extent_ref[home * members + n]
            start = (
                center_ref[home * members + n]
                - home * depth
                - lax.shift_right_logical(extent, 1)
                + (slot - 1) * depth
            )
            begin = jnp.where(member == n, start, begin)
            end = jnp.where(member == n, start + extent, end)
        limits[slot, 0] = begin
        limits[slot, 1] = end

    for step in (*direct, *relayed):
        send(1, step)
    for step in relayed:
        arrived(0, targets[step])
        relay(step)
    pot_copy.wait_recv()

    at_lane = lax.broadcasted_iota(jnp.int32, (members * COMP, 128), 1)
    func = lax.rem(lax.broadcasted_iota(jnp.int32, (members * COMP, 128), 0), per)
    keep = ((at_lane < CY) | (at_lane >= 128 - CY)) == (func < half)

    for role in range(3):
        slot = slots[role]
        for step in direct if role == 0 else range(groups):
            arrived(role, targets[step])

        @pl.loop(0, depth + 2, unroll=(depth + 2) // 2)
        def _(j):
            x = got[role, :, j].reshape(members * COMP, seg)
            turned = jnp.dot(
                order_ref[: members * COMP], x, preferred_element_type=jnp.float32
            ).reshape(COMP, members, seg)
            if role != 1:
                inside = (limits[slot, 0] < j) & (limits[slot, 1] >= j)
                turned = jnp.where(inside[None], turned, 0.0)
            orb[slot, j] = turned.astype(jnp.bfloat16)

        @pl.loop(0, depth, unroll=8)
        def _(z):
            x = got[role, :, z + 1].reshape(members * COMP, seg)
            fine = jnp.dot(
                order_ref[members * COMP :], x, preferred_element_type=jnp.float32
            ).reshape(COMP, members, seg)
            hx = got_halo[role, :, z].reshape(members * COMP // 2, 128)
            edge = jnp.dot(pick_ref[...], hx, preferred_element_type=jnp.float32)
            edge = jnp.where(keep, edge, 0.0).astype(jnp.bfloat16)
            here = orb[slot, z + 1].reshape(members * COMP, seg)
            term = jnp.dot(here, lap_ref[:seg], preferred_element_type=jnp.float32)
            term += jnp.dot(edge, lap_ref[seg:], preferred_element_type=jnp.float32)
            term = term.reshape(COMP, members, seg)
            pot = got_pot[z].astype(jnp.float32)
            vals = [fine[k] * pot[k : k + 1] for k in range(COMP)]
            width = 1
            while width < COMP:
                vals = [
                    vals[k] + vals[k + width] if not k & width else vals[k - width] - vals[k]
                    for k in range(COMP)
                ]
                width *= 2
            inside = (limits[slot, 0] <= z) & (limits[slot, 1] > z)
            for c in range(COMP):
                beside = orb[slot, z, c].astype(jnp.float32) + orb[slot, z + 2, c].astype(
                    jnp.float32
                )
                total = term[c] - 0.5 * beside + vals[c] * (1.0 / COMP)
                app[slot, z, c] = jnp.where(inside, total, 0.0).astype(jnp.bfloat16)

    def gram(z, acc):
        for c in range(COMP):
            columns = jnp.concatenate([orb[k, z + 1, c] for k in range(3)], 0)
            images = jnp.concatenate([app[k, z, c] for k in range(3)], 0)
            acc += lax.dot_general(
                jnp.concatenate([columns, images], 0),
                columns,
                (((1,), (1,)), ((), ())),
                preferred_element_type=jnp.float32,
            )
        return acc

    wide = 3 * members
    rows[...] = jnp.zeros_like(rows)
    acc = lax.fori_loop(0, depth, gram, jnp.zeros((2 * wide, wide), jnp.float32), unroll=4)
    for slot in range(3):
        for g in range(groups):
            at = slot * members + g * per
            rows[slot, g, 0:per, 0:wide] = acc[at : at + per]
            rows[slot, g, per : 2 * per, 0:wide] = acc[wide + at : wide + at + per]

    for step, to in enumerate(targets):
        for role in (2, 1, 0):
            slot = slots[role]
            move(
                role,
                step,
                rows.at[slot, to],
                got_rows.at[slot, me],
                send_rows,
                recv_rows.at[role, me],
                (rows_to[role], to),
            )
    for role in range(3):
        for g in range(groups):
            block = got_rows.at[slots[role], g]
            pltpu.make_async_copy(block, block, recv_rows.at[role, g]).wait()
    parts = []
    for slot in range(3):
        part = got_rows[slot, 0]
        for g in range(1, groups):
            part = part + got_rows[slot, g]
        parts.append(part)
    out_ref[...] = (
        pltpu.roll(parts[0], 2 * members, 1) + pltpu.roll(parts[1], members, 1) + parts[2]
    )
    pot_copy.wait_send()
    for copy in unsent:
        copy.wait_send()


def split_kernel(band_ref, margin_ref, ham_ref):
    per, width = margin_ref.shape
    margin_ref[...] = band_ref[:per, :width]
    ham_ref[...] = band_ref[per:, :width]


def local(slabs, groups, potential, coefficients, box_center, box_extent):
    per, box, comp, cells = coefficients.shape
    depth = potential.shape[0]
    members = groups * per
    seg = cells // groups
    vmem = pl.BlockSpec(memory_space=pltpu.VMEM)
    smem = pl.BlockSpec(memory_space=pltpu.SMEM)
    anywhere = pl.BlockSpec(memory_space=pl.ANY)
    frames = lambda n: pltpu.VMEM((n, groups, depth + 2, per * comp, seg), jnp.bfloat16)
    halos = lambda n: pltpu.VMEM((n, groups, depth, per * comp // 2, 128), jnp.bfloat16)
    sums = pltpu.VMEM((3, groups, 2 * per, 128), jnp.float32)
    dma = pltpu.SemaphoreType.DMA
    band = pl.pallas_call(
        functools.partial(band_kernel, slabs, groups, depth),
        out_shape=jax.ShapeDtypeStruct((2 * per, 128), jnp.float32),
        in_specs=[vmem, anywhere, smem, smem, vmem, vmem, vmem],
        out_specs=vmem,
        scratch_shapes=[
            frames(2),
            halos(2),
            frames(3),
            halos(3),
            pltpu.VMEM((depth, comp, seg), jnp.bfloat16),
            pltpu.VMEM((3, depth + 2, comp, members, seg), jnp.bfloat16),
            pltpu.VMEM((3, depth, comp, members, seg), jnp.bfloat16),
            pltpu.VMEM((3, 2, members, seg), jnp.int32),
            sums,
            sums,
            dma((3, groups)),
            dma((3, groups)),
            dma,
            dma((3, groups)),
            dma((3, groups)),
            dma((3, groups)),
            dma,
            dma((3, groups)),
        ],
        compiler_params=pltpu.CompilerParams(collective_id=0, has_side_effects=True),
        name="band",
    )(coefficients, potential, box_center, box_extent, *matrices(members, per, seg))
    out = jax.ShapeDtypeStruct((per, 5 * members), jnp.float32)
    return pl.pallas_call(
        split_kernel, out_shape=(out, out), in_specs=[vmem], out_specs=(vmem, vmem), name="split"
    )(band)


def solution(mesh):
    return jax.shard_map(
        functools.partial(local, mesh.shape["slab"], mesh.shape["grp"]),
        mesh=mesh,
        in_specs=(P("slab", None, None), P(("slab", "grp"), None, None, None), P(), P()),
        out_specs=(P(("slab", "grp"), None), P(("slab", "grp"), None)),
        check_vma=False,
    )
```
